32 devices in a mesh: gy: 4 (over y, x), gx: 8 (over z, core).
Axes of the slice: x: 2, y: 2, z: 4, core: 2. Of those that a mesh axis runs over, the one named last changes fastest.
Arguments:
- cost_volume: int32 [64, 128, 256], P('gy', 'gx'), may hold values from 0 to 64
- left_image: float32 [64, 128], P('gy', 'gx'), may hold values from -6 to 6
- p_small: int32 [4], replicated, may hold values from 4 to 16
- p_large: int32 [4], replicated, may hold values from 32 to 128
Outputs:
- aggregated: float32 [64, 128, 256], P('gy', 'gx')
The draws below stay inside these ranges and needn't reach their ends.
Inputs may be any that keep to these rules, and one draw needn't show every extreme that they name: `p_small`: every small penalty is below every large penalty.
All inputs are finite; a program needn't handle non-finite values.
Results may differ from the reference program's by a relative error of at most 0.00002.
Values sent between devices are 32-bit elements; how exact they have to be, the bound alone decides.
A program may use at most 64 MiB of HBM per device.

```python
from functools import partial
import jax
import jax.numpy as jnp
from jax import lax

DSP = 256
H = 64
W = 128


def draw_cost_volume(key, part):
    subkeys = jax.random.split(jax.random.fold_in(key, 11), 10)
    row_index = jnp.arange(H, dtype=jnp.int32)[:, None]
    column_index = jnp.arange(W, dtype=jnp.int32)[None, :]
    stripe_span = jax.random.randint(subkeys[0], (), W * 3 // 8, W // 2 + 1, dtype=jnp.int32)
    stripe_start = jax.random.randint(subkeys[1], (), W // 8, W - stripe_span - W // 8 + 1, dtype=jnp.int32)
    band_span = jax.random.randint(subkeys[2], (), H * 3 // 8, H // 2 + 1, dtype=jnp.int32)
    band_start = jax.random.randint(subkeys[3], (), H // 8, H - band_span - H // 8 + 1, dtype=jnp.int32)
    in_stripe = jnp.logical_and(column_index >= stripe_start, column_index < stripe_start + stripe_span)
    in_band = jnp.logical_and(row_index >= band_start, row_index < band_start + band_span)
    untextured = jnp.logical_or(in_stripe, in_band)
    slope_cols = jax.random.randint(subkeys[4], (), -(DSP // 2), DSP // 2 + 1, dtype=jnp.int32)
    slope_rows = jax.random.randint(subkeys[5], (), -(DSP // 2), DSP // 2 + 1, dtype=jnp.int32)
    shift_base = jax.random.randint(subkeys[6], (), 0, DSP, dtype=jnp.int32)
    jitter = jax.random.randint(subkeys[7], (H, W), -1, 2, dtype=jnp.int32)
    surface = jnp.mod(shift_base + slope_cols * column_index // W + slope_rows * row_index // H + jitter, DSP)
    labels = jnp.arange(DSP, dtype=jnp.int32)
    distance = jnp.minimum(jnp.abs(labels[None, None, :] - surface[:, :, None]), 10)
    textured = jnp.minimum(jax.random.randint(subkeys[8], (H, W, DSP), 0, 25, dtype=jnp.int32) + 4 * distance, 64)
    plateau = jax.random.randint(subkeys[9], (H, W), 8, 57, dtype=jnp.int32)
    return jnp.where(untextured[:, :, None], plateau[:, :, None], textured).astype(jnp.int32)


def with_ends(drawn, key, smallest, largest):
    shape = drawn.shape
    place = [jax.random.randint(jax.random.fold_in(key, axis), (), 0, shape[axis]) for axis in range(len(shape))]
    drawn = drawn.at[tuple(place)].set(smallest)
    longest = shape.index(max(shape))
    place[longest] = (place[longest] + 1) % shape[longest]
    return drawn.at[tuple(place)].set(largest)


def steps_of(own_key, extent, cuts, least, top_value):
    gain, own = 1.0, jax.random.fold_in(own_key, 6)
    for axis_at, parts in cuts:
        steps = jnp.exp(jax.random.uniform(jax.random.fold_in(own, axis_at), (parts,), jnp.float32, least / len(cuts), top_value / len(cuts)))
        gain = gain * jnp.repeat(steps, extent[axis_at] // parts).reshape([-1 if axis == axis_at else 1 for axis in range(len(extent))])
    return gain


def gaussian(own_key, dims, spread, limit, shards=(), kind=jnp.bfloat16):
    gain = steps_of(own_key, dims, shards, -0.22, 0.18) if shards else 1.0
    array = jax.random.normal(own_key, dims, jnp.float32) * spread * gain
    return jnp.minimum(jnp.maximum(array, -limit), limit).astype(kind)


def setup_inputs(seed: int = 0) -> dict:
    key_list = jax.random.split(jax.random.key(seed), 5)
    cost_volume = draw_cost_volume(jax.random.fold_in(key_list[4], 71), 0)
    left_image = gaussian(key_list[1], (H, W), 1.0, 6.0, ((0, 4), (1, 8)), jnp.float32)
    p_small = with_ends(jax.random.randint(key_list[2], (4,), 4, 17), jax.random.fold_in(key_list[2], 1), 4, 16).astype(jnp.int32)
    p_large = with_ends(jax.random.randint(key_list[3], (4,), 32, 129), jax.random.fold_in(key_list[3], 1), 32, 128).astype(jnp.int32)
    return {"cost_volume": cost_volume, "left_image": left_image, "p_small": p_small, "p_large": p_large}


FAR = 1.0e30
GRADIENT_GAIN = 4.0
OUT_SCALE = 1.0 / 256.0


def advance(previous, inputs, penalty_one):
    cost_line, large_line = inputs
    lowest = jnp.min(previous, axis=-1, keepdims=True)
    padded = jnp.pad(previous, ((0, 0), (1, 1)), constant_values=FAR)
    neighbour = jnp.minimum(padded[:, :-2], padded[:, 2:]) + penalty_one
    chosen = jnp.minimum(jnp.minimum(previous, neighbour), lowest + large_line[:, None])
    updated = cost_line.astype(jnp.float32) + chosen - lowest
    return updated, updated


def sweep(cost_lines, large_lines, penalty_one, start, backward):
    boundary, path_part = lax.scan(partial(advance, penalty_one=penalty_one), start, (cost_lines, large_lines), reverse=backward)
    return path_part, boundary


def adaptive(penalty_one, penalty_two, step_diff):
    return penalty_one + (penalty_two - penalty_one) / (1.0 + GRADIENT_GAIN * jnp.abs(step_diff))


def reference(cost_volume, left_image, p_small, p_large):
    padded = jnp.pad(left_image, 1)
    middle = padded[1:-1, 1:-1]
    small_pens = p_small.astype(jnp.float32)
    large_pens = p_large.astype(jnp.float32)
    penalty_right = adaptive(small_pens[0], large_pens[0], middle - padded[1:-1, :-2]).T
    penalty_left = adaptive(small_pens[1], large_pens[1], middle - padded[1:-1, 2:]).T
    penalty_down = adaptive(small_pens[2], large_pens[2], middle - padded[:-2, 1:-1])
    penalty_up = adaptive(small_pens[3], large_pens[3], middle - padded[2:, 1:-1])
    disparities = cost_volume.shape[2]
    crossed = jnp.transpose(cost_volume, (1, 0, 2))
    start_rows = jnp.zeros((crossed.shape[1], disparities), jnp.float32)
    start_cols = jnp.zeros((cost_volume.shape[1], disparities), jnp.float32)
    path_right, _ = sweep(crossed, penalty_right, small_pens[0], start_rows, False)
    path_left, _ = sweep(crossed, penalty_left, small_pens[1], start_rows, True)
    across = path_right + path_left
    path_down, _ = sweep(cost_volume, penalty_down, small_pens[2], start_cols, False)
    path_up, _ = sweep(cost_volume, penalty_up, small_pens[3], start_cols, True)
    down_total = path_down + path_up
    return (down_total + jnp.transpose(across, (1, 0, 2))) * OUT_SCALE
```

```python
import functools

import jax
import jax.numpy as jnp
from jax import lax
from jax.experimental import pallas as pl
from jax.experimental.pallas import tpu as pltpu
from jax.sharding import PartitionSpec as P

FAR = 1e30
GRADIENT_GAIN = 4.0
OUT_SCALE = 1.0 / 256.0
LANES = 128
SUBLANES = 8
MESH = pl.DeviceIdType.MESH


def tree_min(parts):
    parts = list(parts)
    while len(parts) > 1:
        pairs = [jnp.minimum(a, b) for a, b in zip(parts[::2], parts[1::2])]
        parts = pairs + ([parts[-1]] if len(parts) % 2 else [])
    return parts[0]


def all_sublanes_min(x):
    for by in (4, 2, 1):
        x = jnp.minimum(x, pltpu.roll(x, by, 0))
    return x


def kernel(
    rows,
    cols,
    cost_ref,
    image_ref,
    small_ref,
    large_ref,
    out_ref,
    staged,
    totals,
    costs,
    paths,
    turned,
    large_lines,
    image_lines,
    outbox,
    inbox,
    edge_out,
    edge_in,
    send_sems,
    recv_sems,
    edge_send_sems,
    edge_recv_sems,
    local_sems,
):
    disparities = cost_ref.shape[1]
    nv = disparities // SUBLANES
    nx, ny = lax.axis_size("gx"), lax.axis_size("gy")
    ix, iy = lax.axis_index("gx"), lax.axis_index("gy")
    lines = (rows, rows, cols, cols)
    lengths = (cols, cols, rows, rows)
    backward = (False, True, False, True)
    targets = (
        {"gx": ix + 1},
        {"gx": ix - 1},
        {"gy": iy + 1},
        {"gy": iy - 1},
    )
    has_next = (ix < nx - 1, ix > 0, iy < ny - 1, iy > 0)
    has_prev = (ix > 0, ix < nx - 1, iy > 0, iy < ny - 1)

    halves = disparities // LANES

    def cost_copy(h):
        return pltpu.make_async_copy(
            cost_ref.at[:, pl.ds(h * LANES, LANES)], staged.at[h], local_sems.at[h]
        )

    def total_copy(h):
        return pltpu.make_async_copy(
            totals.at[h], out_ref.at[:, pl.ds(h * LANES, LANES)], local_sems.at[h]
        )

    for h in range(halves):
        cost_copy(h).start()

    barrier = pltpu.get_barrier_semaphore()
    for k in range(4):

        @pl.when(has_next[k])
        def _(k=k):
            pl.semaphore_signal(barrier, inc=1, device_id=targets[k], device_id_type=MESH)

    neighbours = sum(jnp.where(flag, 1, 0) for flag in has_next)

    image = image_ref[...]
    image_lines[...] = jnp.zeros_like(image_lines)
    image_lines[0, :cols, :rows] = image.T
    image_lines[1, :rows, :cols] = image
    edge_out[...] = jnp.zeros_like(edge_out)
    for k in range(4):
        last = 0 if backward[k] else lengths[k] - 1
        edge_out[k, 0:1, :] = image_lines[k // 2, last : last + 1, :]
    pl.semaphore_wait(barrier, neighbours)

    def edge_copy(k):
        return pltpu.make_async_remote_copy(
            src_ref=edge_out.at[k],
            dst_ref=edge_in.at[k],
            send_sem=edge_send_sems.at[k],
            recv_sem=edge_recv_sems.at[k],
            device_id=targets[k],
            device_id_type=MESH,
        )

    def path_copy(k):
        return pltpu.make_async_remote_copy(
            src_ref=outbox.at[k],
            dst_ref=inbox.at[k],
            send_sem=send_sems.at[k],
            recv_sem=recv_sems.at[k],
            device_id=targets[k],
            device_id_type=MESH,
        )

    for k in range(4):

        @pl.when(has_next[k])
        def _(k=k):
            edge_copy(k).start()

    for h in range(halves):
        cost_copy(h).wait()

    def turn_in(axis, line, at, count):
        for h in range(halves):
            block = staged[h, at, :].astype(jnp.float32)
            turned[h * LANES : (h + 1) * LANES, :count] = block.T
        for v in range(nv):
            costs[axis, line, v] = turned[pl.ds(v, SUBLANES, stride=nv), :]

    def turn_across(line, carry):
        turn_in(0, line, pl.ds(line, rows, stride=cols), rows)
        return carry

    def turn_down(line, carry):
        turn_in(1, line, pl.ds(pl.multiple_of(line * cols, cols), cols), cols)
        return carry

    lax.fori_loop(0, cols, turn_across, 0)
    lax.fori_loop(0, rows, turn_down, 0)

    sub = lax.broadcasted_iota(jnp.int32, (SUBLANES, LANES), 0)
    lane = lax.broadcasted_iota(jnp.int32, (SUBLANES, LANES), 1)

    def task(k):
        axis = k // 2
        length, width = lengths[k], lines[k]
        group = LANES // width
        small = small_ref[k].astype(jnp.float32)
        large = large_ref[k].astype(jnp.float32)
        own = image_lines[axis, :length, :]

        @pl.when(has_prev[k])
        def _():
            edge_copy(k).wait_recv()

        @pl.when(jnp.logical_not(has_prev[k]))
        def _():
            edge_in[k] = jnp.zeros((SUBLANES, LANES), jnp.float32)
            inbox[k] = jnp.zeros(inbox.shape[1:], jnp.float32)

        edge = edge_in[k, 0:1, :]
        if backward[k]:
            before = jnp.concatenate([own[1:], edge], axis=0)
        else:
            before = jnp.concatenate([edge, own[:-1]], axis=0)
        large_lines[k] = small + (large - small) / (1.0 + GRADIENT_GAIN * jnp.abs(own - before))

        @pl.when(has_prev[k])
        def _():
            path_copy(k).wait_recv()

        state = []
        for v in range(nv):
            packed = inbox[k, v // group]
            shift = (v % group) * width
            state.append(pltpu.roll(packed, LANES - shift, 1) if shift else packed)

        def step(index, state):
            line = length - 1 - index if backward[k] else index
            capped = large_lines[k, pl.ds(line, SUBLANES, stride=0), :]
            lowest = all_sublanes_min(tree_min(state))
            under = jnp.where(sub == 0, FAR, pltpu.roll(state[-1], 1, 0))
            over = jnp.where(sub == SUBLANES - 1, FAR, pltpu.roll(state[0], SUBLANES - 1, 0))
            fresh = []
            for v in range(nv):
                low = state[v - 1] if v else under
                high = state[v + 1] if v < nv - 1 else over
                near = jnp.minimum(state[v], jnp.minimum(low, high) + small)
                value = costs[axis, line, v] + jnp.minimum(near - lowest, capped)
                paths[k, line, v] = value
                fresh.append(value)
            return tuple(fresh)

        state = lax.fori_loop(0, length, step, tuple(state))

        @pl.when(has_next[k])
        def _():
            for slot in range(nv // group):
                packed = state[slot * group]
                for g in range(1, group):
                    moved = pltpu.roll(state[slot * group + g], g * width, 1)
                    packed = jnp.where(lane >= g * width, moved, packed)
                outbox[k, slot] = packed
            path_copy(k).start()

    def turn_out(k, line, count):
        for v in range(nv):
            total = paths[k, line, v] + paths[k + 1, line, v]
            turned[pl.ds(v, SUBLANES, stride=nv), :] = total
        return [
            turned[h * LANES : (h + 1) * LANES, :count].T * OUT_SCALE for h in range(halves)
        ]

    def down_total(line, carry):
        at = pl.ds(pl.multiple_of(line * cols, cols), cols)
        for h, part in enumerate(turn_out(2, line, cols)):
            totals[h, at, :] = part
        return carry

    def across_total(line, carry):
        at = pl.ds(line, rows, stride=cols)
        for h, part in enumerate(turn_out(0, line, rows)):
            totals[h, at, :] = totals[h, at, :] + part
        return carry

    low_turn = jnp.minimum(ix, nx - 1 - ix)
    high_turn = jnp.maximum(ix, nx - 1 - ix)

    def one_turn(turn, carry):
        pl.when(turn == ix)(lambda: task(0))
        pl.when(turn == nx - 1 - ix)(lambda: task(1))
        taken = jnp.logical_or(turn == low_turn, turn == high_turn)
        used = jnp.where(low_turn < turn, 1, 0) + jnp.where(high_turn < turn, 1, 0)
        free = jnp.where(taken, -1, turn - used)
        pl.when(free == iy)(lambda: task(2))
        pl.when(free == ny - 1 - iy)(lambda: task(3))

        @pl.when(free == ny)
        def _():
            lax.fori_loop(0, rows, down_total, 0)

        return carry

    lax.fori_loop(0, max(nx, ny + 3), one_turn, 0)
    lax.fori_loop(0, cols, across_total, 0)
    for h in range(halves):
        total_copy(h).start()
    for h in range(halves):
        total_copy(h).wait()

    for k in range(4):

        @pl.when(has_next[k])
        def _(k=k):
            edge_copy(k).wait_send()
            path_copy(k).wait_send()


def on_device(cost_volume, left_image, p_small, p_large):
    rows, cols, disparities = cost_volume.shape
    nv = disparities // SUBLANES
    longest = max(rows, cols)
    packed = nv * longest // LANES
    halves = disparities // LANES
    hbm = pl.BlockSpec(memory_space=pl.ANY)
    vmem = pl.BlockSpec(memory_space=pltpu.VMEM)
    smem = pl.BlockSpec(memory_space=pltpu.SMEM)
    total = pl.pallas_call(
        functools.partial(kernel, rows, cols),
        out_shape=jax.ShapeDtypeStruct((rows * cols, disparities), jnp.float32),
        in_specs=[hbm, vmem, smem, smem],
        out_specs=hbm,
        scratch_shapes=[
            pltpu.VMEM((halves, rows * cols, LANES), jnp.int32),
            pltpu.VMEM((halves, rows * cols, LANES), jnp.float32),
            pltpu.VMEM((2, longest, nv, SUBLANES, LANES), jnp.float32),
            pltpu.VMEM((4, longest, nv, SUBLANES, LANES), jnp.float32),
            pltpu.VMEM((disparities, LANES), jnp.float32),
            pltpu.VMEM((4, longest, LANES), jnp.float32),
            pltpu.VMEM((2, longest, LANES), jnp.float32),
            pltpu.VMEM((4, packed, SUBLANES, LANES), jnp.float32),
            pltpu.VMEM((4, packed, SUBLANES, LANES), jnp.float32),
            pltpu.VMEM((4, SUBLANES, LANES), jnp.float32),
            pltpu.VMEM((4, SUBLANES, LANES), jnp.float32),
            pltpu.SemaphoreType.DMA((4,)),
            pltpu.SemaphoreType.DMA((4,)),
            pltpu.SemaphoreType.DMA((4,)),
            pltpu.SemaphoreType.DMA((4,)),
            pltpu.SemaphoreType.DMA((halves,)),
        ],
        compiler_params=pltpu.CompilerParams(collective_id=0, has_side_effects=True),
    )(cost_volume.reshape(rows * cols, disparities), left_image, p_small, p_large)
    return total.reshape(rows, cols, disparities)


def solution(mesh):
    in_specs = (P("gy", "gx", None), P("gy", "gx"), P(), P())
    out_specs = P("gy", "gx", None)
    return jax.shard_map(
        on_device, mesh=mesh, in_specs=in_specs, out_specs=out_specs, check_vma=False
    )
```

```python
import functools

import jax
import jax.numpy as jnp
from jax import lax
from jax.experimental import pallas as pl
from jax.experimental.pallas import tpu as pltpu
from jax.sharding import PartitionSpec as P

FAR = 1e30
GRADIENT_GAIN = 4.0
OUT_SCALE = 1.0 / 256.0
LANES = 128
SUBLANES = 8
BATCH = 4
UNROLL = 2
VMEM_BYTES = 20 << 20
MESH = pl.DeviceIdType.MESH


def tree_min(parts):
    parts = list(parts)
    while len(parts) > 1:
        pairs = [jnp.minimum(a, b) for a, b in zip(parts[::2], parts[1::2])]
        parts = pairs + ([parts[-1]] if len(parts) % 2 else [])
    return parts[0]


def all_sublanes_min(x):
    for by in (4, 2, 1):
        x = jnp.minimum(x, pltpu.roll(x, by, 0))
    return x


def kernel(
    rows,
    cols,
    cost_ref,
    image_ref,
    small_ref,
    large_ref,
    out_ref,
    staged,
    totals,
    costs,
    paths,
    turned,
    large_lines,
    image_lines,
    outbox,
    inbox,
    edge_out,
    edge_in,
    send_sems,
    recv_sems,
    edge_send_sems,
    edge_recv_sems,
    local_sems,
):
    disparities = cost_ref.shape[1]
    nv = disparities // SUBLANES
    nx, ny = lax.axis_size("gx"), lax.axis_size("gy")
    ix, iy = lax.axis_index("gx"), lax.axis_index("gy")
    lines = (rows, rows, cols, cols)
    lengths = (cols, cols, rows, rows)
    backward = (False, True, False, True)
    targets = (
        {"gx": ix + 1},
        {"gx": ix - 1},
        {"gy": iy + 1},
        {"gy": iy - 1},
    )
    has_next = (ix < nx - 1, ix > 0, iy < ny - 1, iy > 0)
    has_prev = (ix > 0, ix < nx - 1, iy > 0, iy < ny - 1)

    halves = disparities // LANES

    def cost_copy(h):
        return pltpu.make_async_copy(
            cost_ref.at[:, pl.ds(h * LANES, LANES)], staged.at[h], local_sems.at[h]
        )

    for h in range(halves):
        cost_copy(h).start()

    barrier = pltpu.get_barrier_semaphore()
    for k in range(4):

        @pl.when(has_next[k])
        def _(k=k):
            pl.semaphore_signal(barrier, inc=1, device_id=targets[k], device_id_type=MESH)

    neighbours = sum(jnp.where(flag, 1, 0) for flag in has_next)

    image = image_ref[...]
    image_lines[...] = jnp.zeros_like(image_lines)
    image_lines[0, :cols, :rows] = image.T
    image_lines[1, :rows, :cols] = image
    edge_out[...] = jnp.zeros_like(edge_out)
    for k in range(4):
        last = 0 if backward[k] else lengths[k] - 1
        edge_out[k, 0:1, :] = image_lines[k // 2, last : last + 1, :]
    pl.semaphore_wait(barrier, neighbours)

    def edge_copy(k):
        return pltpu.make_async_remote_copy(
            src_ref=edge_out.at[k],
            dst_ref=edge_in.at[k],
            send_sem=edge_send_sems.at[k],
            recv_sem=edge_recv_sems.at[k],
            device_id=targets[k],
            device_id_type=MESH,
        )

    def path_copy(k):
        return pltpu.make_async_remote_copy(
            src_ref=outbox.at[k],
            dst_ref=inbox.at[k],
            send_sem=send_sems.at[k],
            recv_sem=recv_sems.at[k],
            device_id=targets[k],
            device_id_type=MESH,
        )

    for k in range(4):

        @pl.when(has_next[k])
        def _(k=k):
            edge_copy(k).start()

    for h in range(halves):
        cost_copy(h).wait()

    def turn_in(slot, axis, line, at, count):
        for h in range(halves):
            block = staged[h, at, :].astype(jnp.float32)
            turned[slot, h * LANES : (h + 1) * LANES, :count] = block.T
        for v in range(nv):
            costs[axis, line, v] = turned[slot, pl.ds(v, SUBLANES, stride=nv), :]

    def turn_across(index, carry):
        for slot in range(BATCH):
            line = index * BATCH + slot
            turn_in(slot, 0, line, pl.ds(line, rows, stride=cols), rows)
        return carry

    def turn_down(index, carry):
        for slot in range(BATCH):
            line = index * BATCH + slot
            turn_in(slot, 1, line, pl.ds(pl.multiple_of(line * cols, cols), cols), cols)
        return carry

    lax.fori_loop(0, cols // BATCH, turn_across, 0)

    sub = lax.broadcasted_iota(jnp.int32, (SUBLANES, LANES), 0)
    lane = lax.broadcasted_iota(jnp.int32, (SUBLANES, LANES), 1)

    def task(k):
        axis = k // 2
        length, width = lengths[k], lines[k]
        group = LANES // width
        small = small_ref[k].astype(jnp.float32)
        large = large_ref[k].astype(jnp.float32)
        own = image_lines[axis, :length, :]

        @pl.when(has_prev[k])
        def _():
            edge_copy(k).wait_recv()

        @pl.when(jnp.logical_not(has_prev[k]))
        def _():
            edge_in[k] = jnp.zeros((SUBLANES, LANES), jnp.float32)
            inbox[k] = jnp.zeros(inbox.shape[1:], jnp.float32)

        edge = edge_in[k, 0:1, :]
        if backward[k]:
            before = jnp.concatenate([own[1:], edge], axis=0)
        else:
            before = jnp.concatenate([edge, own[:-1]], axis=0)
        large_lines[k] = small + (large - small) / (1.0 + GRADIENT_GAIN * jnp.abs(own - before))

        @pl.when(has_prev[k])
        def _():
            path_copy(k).wait_recv()

        state = []
        for v in range(nv):
            packed = inbox[k, v // group]
            shift = (v % group) * width
            state.append(pltpu.roll(packed, LANES - shift, 1) if shift else packed)

        def step(index, state):
            line = length - 1 - index if backward[k] else index
            capped = large_lines[k, pl.ds(line, SUBLANES, stride=0), :]
            lowest = all_sublanes_min(tree_min(state))
            under = jnp.where(sub == 0, FAR, pltpu.roll(state[-1], 1, 0))
            over = jnp.where(sub == SUBLANES - 1, FAR, pltpu.roll(state[0], SUBLANES - 1, 0))
            fresh = []
            for v in range(nv):
                low = state[v - 1] if v else under
                high = state[v + 1] if v < nv - 1 else over
                near = jnp.minimum(state[v], jnp.minimum(low, high) + small)
                value = costs[axis, line, v] + jnp.minimum(near - lowest, capped)
                paths[k, line, v] = value
                fresh.append(value)
            return tuple(fresh)

        def steps(index, state):
            for part in range(UNROLL):
                state = step(index * UNROLL + part, state)
            return state

        state = lax.fori_loop(0, length // UNROLL, steps, tuple(state))

        @pl.when(has_next[k])
        def _():
            for slot in range(nv // group):
                packed = state[slot * group]
                for g in range(1, group):
                    moved = pltpu.roll(state[slot * group + g], g * width, 1)
                    packed = jnp.where(lane >= g * width, moved, packed)
                outbox[k, slot] = packed
            path_copy(k).start()

    def turn_out(slot, k, line, count):
        for v in range(nv):
            total = paths[k, line, v] + paths[k + 1, line, v]
            turned[slot, pl.ds(v, SUBLANES, stride=nv), :] = total
        return [turned[slot, h * LANES : (h + 1) * LANES, :count].T for h in range(halves)]

    def down_total(index, carry):
        for slot in range(BATCH):
            line = index * BATCH + slot
            at = pl.ds(pl.multiple_of(line * cols, cols), cols)
            for h, part in enumerate(turn_out(slot, 2, line, cols)):
                totals[h, at, :] = part
        return carry

    def across_total(index, carry):
        for slot in range(BATCH):
            line = index * BATCH + slot
            at = pl.ds(line, rows, stride=cols)
            for h, part in enumerate(turn_out(slot, 0, line, rows)):
                totals[h, at, :] = totals[h, at, :] + part
        return carry

    low_turn = jnp.minimum(ix, nx - 1 - ix)
    high_turn = jnp.maximum(ix, nx - 1 - ix)
    spare = jnp.where(low_turn >= 3, low_turn - 1, 2 * nx + 2 * ny)

    def one_turn(turn, carry):
        pl.when(turn == ix)(lambda: task(0))
        pl.when(turn == nx - 1 - ix)(lambda: task(1))
        taken = jnp.logical_or(turn == low_turn, turn == high_turn)
        taken = jnp.logical_or(taken, turn == spare)
        used = sum(jnp.where(at < turn, 1, 0) for at in (low_turn, high_turn, spare))
        free = jnp.where(taken, -1, turn - used)
        pl.when(free == 0)(lambda: lax.fori_loop(0, rows // BATCH, turn_down, None))
        pl.when(free == iy)(lambda: task(2))
        pl.when(free == ny - 1 - iy)(lambda: task(3))
        pl.when(free == ny)(lambda: lax.fori_loop(0, rows // BATCH, down_total, None))
        return carry

    lax.fori_loop(0, max(nx, ny + 4), one_turn, 0)
    lax.fori_loop(0, cols // BATCH, across_total, 0)
    for h in range(halves):
        out_ref[:, h * LANES : (h + 1) * LANES] = totals[h] * OUT_SCALE

    for k in range(4):

        @pl.when(has_next[k])
        def _(k=k):
            edge_copy(k).wait_send()
            path_copy(k).wait_send()


def on_device(cost_volume, left_image, p_small, p_large):
    rows, cols, disparities = cost_volume.shape
    nv = disparities // SUBLANES
    longest = max(rows, cols)
    packed = nv * longest // LANES
    halves = disparities // LANES
    hbm = pl.BlockSpec(memory_space=pl.ANY)
    vmem = pl.BlockSpec(memory_space=pltpu.VMEM)
    smem = pl.BlockSpec(memory_space=pltpu.SMEM)
    total = pl.pallas_call(
        functools.partial(kernel, rows, cols),
        out_shape=jax.ShapeDtypeStruct((rows * cols, disparities), jnp.float32),
        in_specs=[hbm, vmem, smem, smem],
        out_specs=vmem,
        scratch_shapes=[
            pltpu.VMEM((halves, rows * cols, LANES), jnp.int32),
            pltpu.VMEM((halves, rows * cols, LANES), jnp.float32),
            pltpu.VMEM((2, longest, nv, SUBLANES, LANES), jnp.float32),
            pltpu.VMEM((4, longest, nv, SUBLANES, LANES), jnp.float32),
            pltpu.VMEM((BATCH, disparities, LANES), jnp.float32),
            pltpu.VMEM((4, longest, LANES), jnp.float32),
            pltpu.VMEM((2, longest, LANES), jnp.float32),
            pltpu.VMEM((4, packed, SUBLANES, LANES), jnp.float32),
            pltpu.VMEM((4, packed, SUBLANES, LANES), jnp.float32),
            pltpu.VMEM((4, SUBLANES, LANES), jnp.float32),
            pltpu.VMEM((4, SUBLANES, LANES), jnp.float32),
            pltpu.SemaphoreType.DMA((4,)),
            pltpu.SemaphoreType.DMA((4,)),
            pltpu.SemaphoreType.DMA((4,)),
            pltpu.SemaphoreType.DMA((4,)),
            pltpu.SemaphoreType.DMA((halves,)),
        ],
        compiler_params=pltpu.CompilerParams(
            collective_id=0, has_side_effects=True, vmem_limit_bytes=VMEM_BYTES
        ),
    )(cost_volume.reshape(rows * cols, disparities), left_image, p_small, p_large)
    return total.reshape(rows, cols, disparities)


def solution(mesh):
    in_specs = (P("gy", "gx", None), P("gy", "gx"), P(), P())
    out_specs = P("gy", "gx", None)
    return jax.shard_map(
        on_device, mesh=mesh, in_specs=in_specs, out_specs=out_specs, check_vma=False
    )
```

```python
import functools

import jax
import jax.numpy as jnp
from jax import lax
from jax.experimental import pallas as pl
from jax.experimental.pallas import tpu as pltpu
from jax.sharding import PartitionSpec as P

FAR = 1e30
GRADIENT_GAIN = 4.0
OUT_SCALE = 1.0 / 256.0
LANES = 128
SUBLANES = 8
BATCH = 4
UNROLL = 2
VMEM_BYTES = 20 << 20
MESH = pl.DeviceIdType.MESH


def tree_min(parts):
    parts = list(parts)
    while len(parts) > 1:
        pairs = [jnp.minimum(a, b) for a, b in zip(parts[::2], parts[1::2])]
        parts = pairs + ([parts[-1]] if len(parts) % 2 else [])
    return parts[0]


def all_sublanes_min(x):
    for by in (4, 2, 1):
        x = jnp.minimum(x, pltpu.roll(x, by, 0))
    return x


def kernel(
    rows,
    cols,
    cost_ref,
    image_hbm,
    small_hbm,
    large_hbm,
    out_ref,
    image_ref,
    small_ref,
    large_ref,
    staged,
    ordered,
    order,
    totals,
    costs,
    paths,
    large_lines,
    image_lines,
    outbox,
    inbox,
    edge_out,
    edge_in,
    send_sems,
    recv_sems,
    edge_send_sems,
    edge_recv_sems,
    local_sems,
):
    disparities = cost_ref.shape[1]
    nv = disparities // SUBLANES
    nx, ny = lax.axis_size("gx"), lax.axis_size("gy")
    ix, iy = lax.axis_index("gx"), lax.axis_index("gy")
    lines = (rows, rows, cols, cols)
    lengths = (cols, cols, rows, rows)
    backward = (False, True, False, True)
    targets = (
        {"gx": ix + 1},
        {"gx": ix - 1},
        {"gy": iy + 1},
        {"gy": iy - 1},
    )
    has_next = (ix < nx - 1, ix > 0, iy < ny - 1, iy > 0)
    has_prev = (ix > 0, ix < nx - 1, iy > 0, iy < ny - 1)

    halves = disparities // LANES

    def cost_copy(h):
        return pltpu.make_async_copy(
            cost_ref.at[:, pl.ds(h * LANES, LANES)], staged.at[h], local_sems.at[h]
        )

    small_copies = [
        pltpu.make_async_copy(source, target, local_sems.at[halves + at])
        for at, (source, target) in enumerate(
            ((image_hbm, image_ref), (small_hbm, small_ref), (large_hbm, large_ref))
        )
    ]
    for h in range(halves):
        cost_copy(h).start()
    for copy in small_copies:
        copy.start()

    barrier = pltpu.get_barrier_semaphore()
    for k in range(4):

        @pl.when(has_next[k])
        def _(k=k):
            pl.semaphore_signal(barrier, inc=1, device_id=targets[k], device_id_type=MESH)

    neighbours = sum(jnp.where(flag, 1, 0) for flag in has_next)

    shape = (disparities, disparities)
    source = lax.broadcasted_iota(jnp.int32, shape, 0)
    target = lax.broadcasted_iota(jnp.int32, shape, 1)
    wanted = target // SUBLANES + nv * (target % SUBLANES)
    order[...] = jnp.where(source == wanted, 1.0, 0.0).astype(jnp.bfloat16)

    for copy in small_copies:
        copy.wait()
    image = image_ref[...]
    image_lines[...] = jnp.zeros_like(image_lines)
    image_lines[0, :cols, :rows] = image.T
    image_lines[1, :rows, :cols] = image
    edge_out[...] = jnp.zeros_like(edge_out)
    for k in range(4):
        last = 0 if backward[k] else lengths[k] - 1
        edge_out[k, 0:1, :] = image_lines[k // 2, last : last + 1, :]
    pl.semaphore_wait(barrier, neighbours)

    def edge_copy(k):
        return pltpu.make_async_remote_copy(
            src_ref=edge_out.at[k],
            dst_ref=edge_in.at[k],
            send_sem=edge_send_sems.at[k],
            recv_sem=edge_recv_sems.at[k],
            device_id=targets[k],
            device_id_type=MESH,
        )

    def path_copy(k):
        return pltpu.make_async_remote_copy(
            src_ref=outbox.at[k],
            dst_ref=inbox.at[k],
            send_sem=send_sems.at[k],
            recv_sem=recv_sems.at[k],
            device_id=targets[k],
            device_id_type=MESH,
        )

    for k in range(4):

        @pl.when(has_next[k])
        def _(k=k):
            edge_copy(k).start()

    for h in range(halves):
        cost_copy(h).wait()

    block = jnp.concatenate([staged[h] for h in range(halves)], axis=1)
    block = block.astype(jnp.float32).astype(jnp.bfloat16)
    block = jnp.dot(block, order[...], preferred_element_type=jnp.float32)
    for h in range(halves):
        ordered[h] = block[:, h * LANES : (h + 1) * LANES]

    def turn_in(axis, line, at, count):
        per = LANES // SUBLANES
        for h in range(halves):
            block = ordered[h, at, :].T.reshape(per, SUBLANES, count)
            costs[axis, line, h * per : (h + 1) * per, :, :count] = block

    def turn_across(index, carry):
        for slot in range(BATCH):
            line = index * BATCH + slot
            turn_in(0, line, pl.ds(line, rows, stride=cols), rows)
        return carry

    def turn_down(index, carry):
        for slot in range(BATCH):
            line = index * BATCH + slot
            turn_in(1, line, pl.ds(pl.multiple_of(line * cols, cols), cols), cols)
        return carry

    lax.fori_loop(0, cols // BATCH, turn_across, 0)

    sub = lax.broadcasted_iota(jnp.int32, (SUBLANES, LANES), 0)
    lane = lax.broadcasted_iota(jnp.int32, (SUBLANES, LANES), 1)

    def task(k):
        axis = k // 2
        length, width = lengths[k], lines[k]
        group = LANES // width
        small = small_ref[k].astype(jnp.float32)
        large = large_ref[k].astype(jnp.float32)
        own = image_lines[axis, :length, :]

        @pl.when(has_prev[k])
        def _():
            edge_copy(k).wait_recv()

        @pl.when(jnp.logical_not(has_prev[k]))
        def _():
            edge_in[k] = jnp.zeros((SUBLANES, LANES), jnp.float32)
            inbox[k] = jnp.zeros(inbox.shape[1:], jnp.float32)

        edge = edge_in[k, 0:1, :]
        if backward[k]:
            before = jnp.concatenate([own[1:], edge], axis=0)
        else:
            before = jnp.concatenate([edge, own[:-1]], axis=0)
        large_lines[k] = small + (large - small) / (1.0 + GRADIENT_GAIN * jnp.abs(own - before))

        @pl.when(has_prev[k])
        def _():
            path_copy(k).wait_recv()

        state = []
        for v in range(nv):
            packed = inbox[k, v // group]
            shift = (v % group) * width
            state.append(pltpu.roll(packed, LANES - shift, 1) if shift else packed)

        def step(index, state):
            line = length - 1 - index if backward[k] else index
            capped = large_lines[k, pl.ds(line, SUBLANES, stride=0), :]
            lowest = all_sublanes_min(tree_min(state))
            under = jnp.where(sub == 0, FAR, pltpu.roll(state[-1], 1, 0))
            over = jnp.where(sub == SUBLANES - 1, FAR, pltpu.roll(state[0], SUBLANES - 1, 0))
            fresh = []
            for v in range(nv):
                low = state[v - 1] if v else under
                high = state[v + 1] if v < nv - 1 else over
                near = jnp.minimum(state[v], jnp.minimum(low, high) + small)
                value = costs[axis, line, v] + jnp.minimum(near - lowest, capped)
                paths[k, line, v] = value
                fresh.append(value)
            return tuple(fresh)

        def steps(index, state):
            for part in range(UNROLL):
                state = step(index * UNROLL + part, state)
            return state

        state = lax.fori_loop(0, length // UNROLL, steps, tuple(state))

        @pl.when(has_next[k])
        def _():
            for slot in range(nv // group):
                packed = state[slot * group]
                for g in range(1, group):
                    moved = pltpu.roll(state[slot * group + g], g * width, 1)
                    packed = jnp.where(lane >= g * width, moved, packed)
                outbox[k, slot] = packed
            path_copy(k).start()

    def turn_out(k, line, count):
        per = LANES // SUBLANES
        parts = []
        for h in range(halves):
            at = pl.ds(h * per, per)
            total = paths[k, line, at] + paths[k + 1, line, at]
            parts.append(total.reshape(LANES, LANES)[:, :count].T)
        return parts

    def down_total(index, carry):
        for slot in range(BATCH):
            line = index * BATCH + slot
            at = pl.ds(pl.multiple_of(line * cols, cols), cols)
            for h, part in enumerate(turn_out(2, line, cols)):
                totals[h, at, :] = part
        return carry

    def across_total(index, carry):
        for slot in range(BATCH):
            line = index * BATCH + slot
            at = pl.ds(line, rows, stride=cols)
            for h, part in enumerate(turn_out(0, line, rows)):
                totals[h, at, :] = totals[h, at, :] + part
        return carry

    low_turn = jnp.minimum(ix, nx - 1 - ix)
    high_turn = jnp.maximum(ix, nx - 1 - ix)
    spare = jnp.where(low_turn >= 3, low_turn - 1, 2 * nx + 2 * ny)

    def one_turn(turn, carry):
        pl.when(turn == ix)(lambda: task(0))
        pl.when(turn == nx - 1 - ix)(lambda: task(1))
        taken = jnp.logical_or(turn == low_turn, turn == high_turn)
        taken = jnp.logical_or(taken, turn == spare)
        used = sum(jnp.where(at < turn, 1, 0) for at in (low_turn, high_turn, spare))
        free = jnp.where(taken, -1, turn - used)
        pl.when(free == 0)(lambda: lax.fori_loop(0, rows // BATCH, turn_down, None))
        pl.when(free == iy)(lambda: task(2))
        pl.when(free == ny - 1 - iy)(lambda: task(3))
        pl.when(free == ny)(lambda: lax.fori_loop(0, rows // BATCH, down_total, None))
        return carry

    lax.fori_loop(0, max(nx, ny + 4), one_turn, 0)
    lax.fori_loop(0, cols // BATCH, across_total, 0)
    rest = jnp.concatenate([totals[h] for h in range(halves)], axis=1) * OUT_SCALE
    result = None
    for part in range(3):
        piece = rest.astype(jnp.bfloat16)
        moved = lax.dot_general(
            piece, order[...], (((1,), (1,)), ((), ())), preferred_element_type=jnp.float32
        )
        result = moved if part == 0 else result + moved
        if part < 2:
            rest = rest - piece.astype(jnp.float32)
    out_ref[...] = result

    for k in range(4):

        @pl.when(has_next[k])
        def _(k=k):
            edge_copy(k).wait_send()
            path_copy(k).wait_send()


def on_device(cost_volume, left_image, p_small, p_large):
    rows, cols, disparities = cost_volume.shape
    nv = disparities // SUBLANES
    longest = max(rows, cols)
    packed = nv * longest // LANES
    halves = disparities // LANES
    hbm = pl.BlockSpec(memory_space=pltpu.HBM)
    vmem = pl.BlockSpec(memory_space=pltpu.VMEM)
    total = pl.pallas_call(
        functools.partial(kernel, rows, cols),
        out_shape=jax.ShapeDtypeStruct((rows * cols, disparities), jnp.float32),
        in_specs=[hbm] * 4,
        out_specs=vmem,
        scratch_shapes=[
            pltpu.VMEM((rows, cols), jnp.float32),
            pltpu.SMEM((4,), jnp.int32),
            pltpu.SMEM((4,), jnp.int32),
            pltpu.VMEM((halves, rows * cols, LANES), jnp.int32),
            pltpu.VMEM((halves, rows * cols, LANES), jnp.float32),
            pltpu.VMEM((disparities, disparities), jnp.bfloat16),
            pltpu.VMEM((halves, rows * cols, LANES), jnp.float32),
            pltpu.VMEM((2, longest, nv, SUBLANES, LANES), jnp.float32),
            pltpu.VMEM((4, longest, nv, SUBLANES, LANES), jnp.float32),
            pltpu.VMEM((4, longest, LANES), jnp.float32),
            pltpu.VMEM((2, longest, LANES), jnp.float32),
            pltpu.VMEM((4, packed, SUBLANES, LANES), jnp.float32),
            pltpu.VMEM((4, packed, SUBLANES, LANES), jnp.float32),
            pltpu.VMEM((4, SUBLANES, LANES), jnp.float32),
            pltpu.VMEM((4, SUBLANES, LANES), jnp.float32),
            pltpu.SemaphoreType.DMA((4,)),
            pltpu.SemaphoreType.DMA((4,)),
            pltpu.SemaphoreType.DMA((4,)),
            pltpu.SemaphoreType.DMA((4,)),
            pltpu.SemaphoreType.DMA((halves + 3,)),
        ],
        compiler_params=pltpu.CompilerParams(
            collective_id=0, has_side_effects=True, vmem_limit_bytes=VMEM_BYTES
        ),
    )(cost_volume.reshape(rows * cols, disparities), left_image, p_small, p_large)
    return total.reshape(rows, cols, disparities)


def solution(mesh):
    in_specs = (P("gy", "gx", None), P("gy", "gx"), P(), P())
    out_specs = P("gy", "gx", None)
    return jax.shard_map(
        on_device, mesh=mesh, in_specs=in_specs, out_specs=out_specs, check_vma=False
    )
```

```python
import functools

import jax
import jax.numpy as jnp
from jax import lax
from jax.experimental import pallas as pl
from jax.experimental.pallas import tpu as pltpu
from jax.sharding import PartitionSpec as P

FAR = 1e30
GRADIENT_GAIN = 4.0
OUT_SCALE = 1.0 / 256.0
LANES = 128
SUBLANES = 8
BATCH = 4
UNROLL = 2
VMEM_BYTES = 20 << 20
MESH = pl.DeviceIdType.MESH


def tree_min(parts):
    parts = list(parts)
    while len(parts) > 1:
        pairs = [jnp.minimum(a, b) for a, b in zip(parts[::2], parts[1::2])]
        parts = pairs + ([parts[-1]] if len(parts) % 2 else [])
    return parts[0]


def all_sublanes_min(x):
    for by in (4, 2, 1):
        x = jnp.minimum(x, pltpu.roll(x, by, 0))
    return x


def kernel(
    rows,
    cols,
    cost_ref,
    image_hbm,
    small_hbm,
    large_hbm,
    out_ref,
    image_ref,
    small_ref,
    large_ref,
    staged,
    ordered,
    order,
    totals,
    costs,
    paths,
    large_lines,
    image_lines,
    outbox,
    inbox,
    edge_out,
    edge_in,
    send_sems,
    recv_sems,
    edge_send_sems,
    edge_recv_sems,
    local_sems,
):
    disparities = cost_ref.shape[1]
    nv = disparities // SUBLANES
    nx, ny = lax.axis_size("gx"), lax.axis_size("gy")
    ix, iy = lax.axis_index("gx"), lax.axis_index("gy")
    lines = (rows, rows, cols, cols)
    lengths = (cols, cols, rows, rows)
    backward = (False, True, False, True)
    targets = (
        {"gx": ix + 1},
        {"gx": ix - 1},
        {"gy": iy + 1},
        {"gy": iy - 1},
    )
    has_next = (ix < nx - 1, ix > 0, iy < ny - 1, iy > 0)
    has_prev = (ix > 0, ix < nx - 1, iy > 0, iy < ny - 1)

    halves = disparities // LANES

    def cost_copy(h):
        return pltpu.make_async_copy(
            cost_ref.at[:, pl.ds(h * LANES, LANES)], staged.at[h], local_sems.at[h]
        )

    small_copies = [
        pltpu.make_async_copy(source, target, local_sems.at[halves + at])
        for at, (source, target) in enumerate(
            ((image_hbm, image_ref), (small_hbm, small_ref), (large_hbm, large_ref))
        )
    ]
    for h in range(halves):
        cost_copy(h).start()
    for copy in small_copies:
        copy.start()

    barrier = pltpu.get_barrier_semaphore()
    for k in range(4):

        @pl.when(has_next[k])
        def _(k=k):
            pl.semaphore_signal(barrier, inc=1, device_id=targets[k], device_id_type=MESH)

    neighbours = sum(jnp.where(flag, 1, 0) for flag in has_next)

    shape = (disparities, disparities)
    source = lax.broadcasted_iota(jnp.int32, shape, 0)
    target = lax.broadcasted_iota(jnp.int32, shape, 1)
    wanted = target // SUBLANES + nv * (target % SUBLANES)
    order[...] = jnp.where(source == wanted, 1.0, 0.0).astype(jnp.bfloat16)

    for copy in small_copies:
        copy.wait()
    image = image_ref[...]
    image_lines[...] = jnp.zeros_like(image_lines)
    image_lines[0, :cols, :rows] = image.T
    image_lines[1, :rows, :cols] = image
    edge_out[...] = jnp.zeros_like(edge_out)
    for k in range(4):
        last = 0 if backward[k] else lengths[k] - 1
        edge_out[k, 0:1, :] = image_lines[k // 2, last : last + 1, :]

    def edge_copy(k):
        return pltpu.make_async_remote_copy(
            src_ref=edge_out.at[k],
            dst_ref=edge_in.at[k],
            send_sem=edge_send_sems.at[k],
            recv_sem=edge_recv_sems.at[k],
            device_id=targets[k],
            device_id_type=MESH,
        )

    def path_copy(k):
        return pltpu.make_async_remote_copy(
            src_ref=outbox.at[k],
            dst_ref=inbox.at[k],
            send_sem=send_sems.at[k],
            recv_sem=recv_sems.at[k],
            device_id=targets[k],
            device_id_type=MESH,
        )

    for h in range(halves):
        cost_copy(h).wait()

    block = jnp.concatenate([staged[h] for h in range(halves)], axis=1)
    block = block.astype(jnp.float32).astype(jnp.bfloat16)
    block = jnp.dot(block, order[...], preferred_element_type=jnp.float32)
    for h in range(halves):
        ordered[h] = block[:, h * LANES : (h + 1) * LANES]

    def turn_in(axis, line, at, count):
        per = LANES // SUBLANES
        for h in range(halves):
            block = ordered[h, at, :].T.reshape(per, SUBLANES, count)
            costs[axis, line, h * per : (h + 1) * per, :, :count] = block

    def turn_across(index, carry):
        for slot in range(BATCH):
            line = index * BATCH + slot
            turn_in(0, line, pl.ds(line, rows, stride=cols), rows)
        return carry

    def turn_down(index, carry):
        for slot in range(BATCH):
            line = index * BATCH + slot
            turn_in(1, line, pl.ds(pl.multiple_of(line * cols, cols), cols), cols)
        return carry

    lax.fori_loop(0, cols // BATCH, turn_across, 0)

    pl.semaphore_wait(barrier, neighbours)
    for k in range(4):

        @pl.when(has_next[k])
        def _(k=k):
            edge_copy(k).start()

    sub = lax.broadcasted_iota(jnp.int32, (SUBLANES, LANES), 0)
    lane = lax.broadcasted_iota(jnp.int32, (SUBLANES, LANES), 1)

    def task(k):
        axis = k // 2
        length, width = lengths[k], lines[k]
        group = LANES // width
        small = small_ref[k].astype(jnp.float32)
        large = large_ref[k].astype(jnp.float32)
        own = image_lines[axis, :length, :]

        @pl.when(has_prev[k])
        def _():
            edge_copy(k).wait_recv()

        @pl.when(jnp.logical_not(has_prev[k]))
        def _():
            edge_in[k] = jnp.zeros((SUBLANES, LANES), jnp.float32)
            inbox[k] = jnp.zeros(inbox.shape[1:], jnp.float32)

        edge = edge_in[k, 0:1, :]
        if backward[k]:
            before = jnp.concatenate([own[1:], edge], axis=0)
        else:
            before = jnp.concatenate([edge, own[:-1]], axis=0)
        large_lines[k] = small + (large - small) / (1.0 + GRADIENT_GAIN * jnp.abs(own - before))

        @pl.when(has_prev[k])
        def _():
            path_copy(k).wait_recv()

        state = []
        for v in range(nv):
            packed = inbox[k, v // group]
            shift = (v % group) * width
            state.append(pltpu.roll(packed, LANES - shift, 1) if shift else packed)

        def step(index, state):
            line = length - 1 - index if backward[k] else index
            capped = large_lines[k, pl.ds(line, SUBLANES, stride=0), :]
            lowest = all_sublanes_min(tree_min(state))
            under = jnp.where(sub == 0, FAR, pltpu.roll(state[-1], 1, 0))
            over = jnp.where(sub == SUBLANES - 1, FAR, pltpu.roll(state[0], SUBLANES - 1, 0))
            fresh = []
            for v in range(nv):
                low = state[v - 1] if v else under
                high = state[v + 1] if v < nv - 1 else over
                near = jnp.minimum(state[v], jnp.minimum(low, high) + small)
                value = costs[axis, line, v] + jnp.minimum(near - lowest, capped)
                paths[k, line, v] = value
                fresh.append(value)
            return tuple(fresh)

        def steps(index, state):
            for part in range(UNROLL):
                state = step(index * UNROLL + part, state)
            return state

        state = lax.fori_loop(0, length // UNROLL, steps, tuple(state))

        @pl.when(has_next[k])
        def _():
            for slot in range(nv // group):
                packed = state[slot * group]
                for g in range(1, group):
                    moved = pltpu.roll(state[slot * group + g], g * width, 1)
                    packed = jnp.where(lane >= g * width, moved, packed)
                outbox[k, slot] = packed
            path_copy(k).start()

    def turn_out(k, line, count):
        per = LANES // SUBLANES
        parts = []
        for h in range(halves):
            at = pl.ds(h * per, per)
            total = paths[k, line, at] + paths[k + 1, line, at]
            parts.append(total.reshape(LANES, LANES)[:, :count].T)
        return parts

    def down_total(index, carry):
        for slot in range(BATCH):
            line = index * BATCH + slot
            at = pl.ds(pl.multiple_of(line * cols, cols), cols)
            for h, part in enumerate(turn_out(2, line, cols)):
                totals[h, at, :] = part
        return carry

    def across_total(index, carry):
        for slot in range(BATCH):
            line = index * BATCH + slot
            at = pl.ds(line, rows, stride=cols)
            for h, part in enumerate(turn_out(0, line, rows)):
                totals[h, at, :] = totals[h, at, :] + part
        return carry

    low_turn = jnp.minimum(ix, nx - 1 - ix)
    high_turn = jnp.maximum(ix, nx - 1 - ix)
    spare = jnp.where(low_turn >= 3, low_turn - 1, 2 * nx + 2 * ny)

    def one_turn(turn, carry):
        pl.when(turn == ix)(lambda: task(0))
        pl.when(turn == nx - 1 - ix)(lambda: task(1))
        taken = jnp.logical_or(turn == low_turn, turn == high_turn)
        taken = jnp.logical_or(taken, turn == spare)
        used = sum(jnp.where(at < turn, 1, 0) for at in (low_turn, high_turn, spare))
        free = jnp.where(taken, -1, turn - used)
        pl.when(free == 0)(lambda: lax.fori_loop(0, rows // BATCH, turn_down, None))
        pl.when(free == iy)(lambda: task(2))
        pl.when(free == ny - 1 - iy)(lambda: task(3))
        pl.when(free == ny)(lambda: lax.fori_loop(0, rows // BATCH, down_total, None))
        return carry

    lax.fori_loop(0, max(nx, ny + 4), one_turn, 0)
    lax.fori_loop(0, cols // BATCH, across_total, 0)
    rest = jnp.concatenate([totals[h] for h in range(halves)], axis=1) * OUT_SCALE
    result = None
    for part in range(3):
        piece = rest.astype(jnp.bfloat16)
        moved = lax.dot_general(
            piece, order[...], (((1,), (1,)), ((), ())), preferred_element_type=jnp.float32
        )
        result = moved if part == 0 else result + moved
        if part < 2:
            rest = rest - piece.astype(jnp.float32)
    out_ref[...] = result

    for k in range(4):

        @pl.when(has_next[k])
        def _(k=k):
            edge_copy(k).wait_send()
            path_copy(k).wait_send()


def on_device(cost_volume, left_image, p_small, p_large):
    rows, cols, disparities = cost_volume.shape
    nv = disparities // SUBLANES
    longest = max(rows, cols)
    packed = nv * longest // LANES
    halves = disparities // LANES
    hbm = pl.BlockSpec(memory_space=pltpu.HBM)
    vmem = pl.BlockSpec(memory_space=pltpu.VMEM)
    total = pl.pallas_call(
        functools.partial(kernel, rows, cols),
        out_shape=jax.ShapeDtypeStruct((rows * cols, disparities), jnp.float32),
        in_specs=[hbm] * 4,
        out_specs=vmem,
        scratch_shapes=[
            pltpu.VMEM((rows, cols), jnp.float32),
            pltpu.SMEM((4,), jnp.int32),
            pltpu.SMEM((4,), jnp.int32),
            pltpu.VMEM((halves, rows * cols, LANES), jnp.int32),
            pltpu.VMEM((halves, rows * cols, LANES), jnp.float32),
            pltpu.VMEM((disparities, disparities), jnp.bfloat16),
            pltpu.VMEM((halves, rows * cols, LANES), jnp.float32),
            pltpu.VMEM((2, longest, nv, SUBLANES, LANES), jnp.float32),
            pltpu.VMEM((4, longest, nv, SUBLANES, LANES), jnp.float32),
            pltpu.VMEM((4, longest, LANES), jnp.float32),
            pltpu.VMEM((2, longest, LANES), jnp.float32),
            pltpu.VMEM((4, packed, SUBLANES, LANES), jnp.float32),
            pltpu.VMEM((4, packed, SUBLANES, LANES), jnp.float32),
            pltpu.VMEM((4, SUBLANES, LANES), jnp.float32),
            pltpu.VMEM((4, SUBLANES, LANES), jnp.float32),
            pltpu.SemaphoreType.DMA((4,)),
            pltpu.SemaphoreType.DMA((4,)),
            pltpu.SemaphoreType.DMA((4,)),
            pltpu.SemaphoreType.DMA((4,)),
            pltpu.SemaphoreType.DMA((halves + 3,)),
        ],
        compiler_params=pltpu.CompilerParams(
            collective_id=0, has_side_effects=True, vmem_limit_bytes=VMEM_BYTES
        ),
    )(
        *(
            pltpu.with_memory_space_constraint(array, pltpu.HBM)
            for array in (
                cost_volume.reshape(rows * cols, disparities),
                left_image,
                p_small,
                p_large,
            )
        )
    )
    return total.reshape(rows, cols, disparities)


def solution(mesh):
    in_specs = (P("gy", "gx", None), P("gy", "gx"), P(), P())
    out_specs = P("gy", "gx", None)
    return jax.shard_map(
        on_device, mesh=mesh, in_specs=in_specs, out_specs=out_specs, check_vma=False
    )
```

```python
import functools

import jax
import jax.numpy as jnp
from jax import lax
from jax.experimental import pallas as pl
from jax.experimental.pallas import tpu as pltpu
from jax.sharding import PartitionSpec as P

FAR = 1e30
GRADIENT_GAIN = 4.0
OUT_SCALE = 1.0 / 256.0
LANES = 128
SUBLANES = 8
BATCH = 4
UNROLL = 2
VMEM_BYTES = 20 << 20
MESH = pl.DeviceIdType.MESH


def tree_min(parts):
    parts = list(parts)
    while len(parts) > 1:
        pairs = [jnp.minimum(a, b) for a, b in zip(parts[::2], parts[1::2])]
        parts = pairs + ([parts[-1]] if len(parts) % 2 else [])
    return parts[0]


def all_sublanes_min(x):
    for by in (4, 2, 1):
        x = jnp.minimum(x, pltpu.roll(x, by, 0))
    return x


def kernel(
    rows,
    cols,
    cost_ref,
    image_hbm,
    small_hbm,
    large_hbm,
    out_ref,
    image_ref,
    small_ref,
    large_ref,
    staged,
    ordered,
    order,
    totals,
    costs,
    paths,
    lowests,
    large_lines,
    image_lines,
    outbox,
    inbox,
    edge_out,
    edge_in,
    send_sems,
    recv_sems,
    edge_send_sems,
    edge_recv_sems,
    local_sems,
):
    disparities = cost_ref.shape[1]
    nv = disparities // SUBLANES
    nx, ny = lax.axis_size("gx"), lax.axis_size("gy")
    ix, iy = lax.axis_index("gx"), lax.axis_index("gy")
    lines = (rows, rows, cols, cols)
    lengths = (cols, cols, rows, rows)
    backward = (False, True, False, True)
    targets = (
        {"gx": ix + 1},
        {"gx": ix - 1},
        {"gy": iy + 1},
        {"gy": iy - 1},
    )
    has_next = (ix < nx - 1, ix > 0, iy < ny - 1, iy > 0)
    has_prev = (ix > 0, ix < nx - 1, iy > 0, iy < ny - 1)

    halves = disparities // LANES

    def cost_copy(h):
        return pltpu.make_async_copy(
            cost_ref.at[:, pl.ds(h * LANES, LANES)], staged.at[h], local_sems.at[h]
        )

    small_copies = [
        pltpu.make_async_copy(source, target, local_sems.at[halves + at])
        for at, (source, target) in enumerate(
            ((image_hbm, image_ref), (small_hbm, small_ref), (large_hbm, large_ref))
        )
    ]
    for h in range(halves):
        cost_copy(h).start()
    for copy in small_copies:
        copy.start()

    barrier = pltpu.get_barrier_semaphore()
    for k in range(4):

        @pl.when(has_next[k])
        def _(k=k):
            pl.semaphore_signal(barrier, inc=1, device_id=targets[k], device_id_type=MESH)

    neighbours = sum(jnp.where(flag, 1, 0) for flag in has_next)

    shape = (disparities, disparities)
    source = lax.broadcasted_iota(jnp.int32, shape, 0)
    target = lax.broadcasted_iota(jnp.int32, shape, 1)
    wanted = target // SUBLANES + nv * (target % SUBLANES)
    order[...] = jnp.where(source == wanted, 1.0, 0.0).astype(jnp.bfloat16)

    for copy in small_copies:
        copy.wait()
    image = image_ref[...]
    image_lines[...] = jnp.zeros_like(image_lines)
    image_lines[0, :cols, :rows] = image.T
    image_lines[1, :rows, :cols] = image
    edge_out[...] = jnp.zeros_like(edge_out)
    for k in range(4):
        last = 0 if backward[k] else lengths[k] - 1
        edge_out[k, 0:1, :] = image_lines[k // 2, last : last + 1, :]

    def edge_copy(k):
        return pltpu.make_async_remote_copy(
            src_ref=edge_out.at[k],
            dst_ref=edge_in.at[k],
            send_sem=edge_send_sems.at[k],
            recv_sem=edge_recv_sems.at[k],
            device_id=targets[k],
            device_id_type=MESH,
        )

    def path_copy(k):
        return pltpu.make_async_remote_copy(
            src_ref=outbox.at[k],
            dst_ref=inbox.at[k],
            send_sem=send_sems.at[k],
            recv_sem=recv_sems.at[k],
            device_id=targets[k],
            device_id_type=MESH,
        )

    for h in range(halves):
        cost_copy(h).wait()

    block = jnp.concatenate([staged[h] for h in range(halves)], axis=1)
    block = block.astype(jnp.float32).astype(jnp.bfloat16)
    block = jnp.dot(block, order[...], preferred_element_type=jnp.float32)
    for h in range(halves):
        ordered[h] = block[:, h * LANES : (h + 1) * LANES]

    def turn_in(axis, line, at, count):
        per = LANES // SUBLANES
        for h in range(halves):
            block = ordered[h, at, :].T.reshape(per, SUBLANES, count)
            costs[axis, line, h * per : (h + 1) * per, :, :count] = block

    def turn_across(index, carry):
        for slot in range(BATCH):
            line = index * BATCH + slot
            turn_in(0, line, pl.ds(line, rows, stride=cols), rows)
        return carry

    def turn_down(index, carry):
        for slot in range(BATCH):
            line = index * BATCH + slot
            turn_in(1, line, pl.ds(pl.multiple_of(line * cols, cols), cols), cols)
        return carry

    lax.fori_loop(0, cols // BATCH, turn_across, 0)

    pl.semaphore_wait(barrier, neighbours)
    for k in range(4):

        @pl.when(has_next[k])
        def _(k=k):
            edge_copy(k).start()

    sub = lax.broadcasted_iota(jnp.int32, (SUBLANES, LANES), 0)
    lane = lax.broadcasted_iota(jnp.int32, (SUBLANES, LANES), 1)

    def turn_back(registers, count):
        per = LANES // SUBLANES
        return [
            jnp.concatenate(registers[h * per : (h + 1) * per], axis=0)[:, :count].T
            for h in range(halves)
        ]

    def task(k, last=False):
        axis = k // 2
        length, width = lengths[k], lines[k]
        group = LANES // width
        small = small_ref[k].astype(jnp.float32)
        large = large_ref[k].astype(jnp.float32)
        own = image_lines[axis, :length, :]

        @pl.when(has_prev[k])
        def _():
            edge_copy(k).wait_recv()

        @pl.when(jnp.logical_not(has_prev[k]))
        def _():
            edge_in[k] = jnp.zeros((SUBLANES, LANES), jnp.float32)
            inbox[k] = jnp.zeros(inbox.shape[1:], jnp.float32)

        edge = edge_in[k, 0:1, :]
        if backward[k]:
            before = jnp.concatenate([own[1:], edge], axis=0)
        else:
            before = jnp.concatenate([edge, own[:-1]], axis=0)
        large_lines[k] = small + (large - small) / (1.0 + GRADIENT_GAIN * jnp.abs(own - before))

        @pl.when(has_prev[k])
        def _():
            path_copy(k).wait_recv()

        state = []
        for v in range(nv):
            packed = inbox[k, v // group]
            shift = (v % group) * width
            state.append(pltpu.roll(packed, LANES - shift, 1) if shift else packed)

        def step(index, state):
            line = length - 1 - index if backward[k] else index
            capped = large_lines[k, pl.ds(line, SUBLANES, stride=0), :]
            lowest = all_sublanes_min(tree_min(state))
            capped = capped + lowest
            under = jnp.where(sub == 0, FAR, pltpu.roll(state[-1], 1, 0))
            over = jnp.where(sub == SUBLANES - 1, FAR, pltpu.roll(state[0], SUBLANES - 1, 0))
            fresh = []
            for v in range(nv):
                low = state[v - 1] if v else under
                high = state[v + 1] if v < nv - 1 else over
                near = jnp.minimum(state[v], jnp.minimum(low, high) + small)
                fresh.append(costs[axis, line, v] + jnp.minimum(near, capped))
            if last:
                above = lowest + lowests[k ^ 1, line]
                both = [fresh[v] + paths[k ^ 1, line, v] - above for v in range(nv)]
                at = pl.ds(line, rows, stride=cols)
                for h, part in enumerate(turn_back(both, rows)):
                    totals[0, h, at, :] = part
            else:
                for v in range(nv):
                    paths[k, line, v] = fresh[v]
            lowests[k, line] = lowest
            return tuple(fresh)

        def steps(index, state):
            for part in range(UNROLL):
                state = step(index * UNROLL + part, state)
            return state

        state = lax.fori_loop(0, length // UNROLL, steps, tuple(state))

        @pl.when(has_next[k])
        def _():
            above = lowests[k, 0 if backward[k] else length - 1]
            sent = [part - above for part in state]
            for slot in range(nv // group):
                packed = sent[slot * group]
                for g in range(1, group):
                    moved = pltpu.roll(sent[slot * group + g], g * width, 1)
                    packed = jnp.where(lane >= g * width, moved, packed)
                outbox[k, slot] = packed
            path_copy(k).start()

    def down_total(index, carry):
        for slot in range(BATCH):
            line = index * BATCH + slot
            at = pl.ds(pl.multiple_of(line * cols, cols), cols)
            above = lowests[2, line] + lowests[3, line]
            both = [paths[2, line, v] + paths[3, line, v] - above for v in range(nv)]
            for h, part in enumerate(turn_back(both, cols)):
                totals[1, h, at, :] = part
        return carry

    right_first = ix <= nx - 1 - ix
    left_first = ix > nx - 1 - ix
    low_turn = jnp.minimum(ix, nx - 1 - ix)
    high_turn = jnp.maximum(ix, nx - 1 - ix)
    spare = jnp.where(low_turn >= 3, low_turn - 1, 2 * nx + 2 * ny)

    def one_turn(turn, carry):
        right_turn, left_turn = turn == ix, turn == nx - 1 - ix
        pl.when(jnp.logical_and(right_turn, right_first))(lambda: task(0))
        pl.when(jnp.logical_and(left_turn, left_first))(lambda: task(1))
        pl.when(jnp.logical_and(right_turn, left_first))(lambda: task(0, last=True))
        pl.when(jnp.logical_and(left_turn, right_first))(lambda: task(1, last=True))
        taken = jnp.logical_or(turn == low_turn, turn == high_turn)
        taken = jnp.logical_or(taken, turn == spare)
        used = sum(jnp.where(at < turn, 1, 0) for at in (low_turn, high_turn, spare))
        free = jnp.where(taken, -1, turn - used)
        pl.when(free == 0)(lambda: lax.fori_loop(0, rows // BATCH, turn_down, None))
        pl.when(free == iy)(lambda: task(2))
        pl.when(free == ny - 1 - iy)(lambda: task(3))
        pl.when(free == ny)(lambda: lax.fori_loop(0, rows // BATCH, down_total, None))
        return carry

    lax.fori_loop(0, max(nx, ny + 4), one_turn, 0)
    rest = jnp.concatenate([totals[0, h] + totals[1, h] for h in range(halves)], axis=1)
    rest = rest * OUT_SCALE
    result = None
    for part in range(3):
        piece = rest.astype(jnp.bfloat16)
        moved = lax.dot_general(
            piece, order[...], (((1,), (1,)), ((), ())), preferred_element_type=jnp.float32
        )
        result = moved if part == 0 else result + moved
        if part < 2:
            rest = rest - piece.astype(jnp.float32)
    out_ref[...] = result

    for k in range(4):

        @pl.when(has_next[k])
        def _(k=k):
            edge_copy(k).wait_send()
            path_copy(k).wait_send()


def on_device(cost_volume, left_image, p_small, p_large):
    rows, cols, disparities = cost_volume.shape
    nv = disparities // SUBLANES
    longest = max(rows, cols)
    packed = nv * longest // LANES
    halves = disparities // LANES
    hbm = pl.BlockSpec(memory_space=pltpu.HBM)
    vmem = pl.BlockSpec(memory_space=pltpu.VMEM)
    total = pl.pallas_call(
        functools.partial(kernel, rows, cols),
        out_shape=jax.ShapeDtypeStruct((rows * cols, disparities), jnp.float32),
        in_specs=[hbm] * 4,
        out_specs=vmem,
        scratch_shapes=[
            pltpu.VMEM((rows, cols), jnp.float32),
            pltpu.SMEM((4,), jnp.int32),
            pltpu.SMEM((4,), jnp.int32),
            pltpu.VMEM((halves, rows * cols, LANES), jnp.int32),
            pltpu.VMEM((halves, rows * cols, LANES), jnp.float32),
            pltpu.VMEM((disparities, disparities), jnp.bfloat16),
            pltpu.VMEM((2, halves, rows * cols, LANES), jnp.float32),
            pltpu.VMEM((2, longest, nv, SUBLANES, LANES), jnp.float32),
            pltpu.VMEM((4, longest, nv, SUBLANES, LANES), jnp.float32),
            pltpu.VMEM((4, longest, SUBLANES, LANES), jnp.float32),
            pltpu.VMEM((4, longest, LANES), jnp.float32),
            pltpu.VMEM((2, longest, LANES), jnp.float32),
            pltpu.VMEM((4, packed, SUBLANES, LANES), jnp.float32),
            pltpu.VMEM((4, packed, SUBLANES, LANES), jnp.float32),
            pltpu.VMEM((4, SUBLANES, LANES), jnp.float32),
            pltpu.VMEM((4, SUBLANES, LANES), jnp.float32),
            pltpu.SemaphoreType.DMA((4,)),
            pltpu.SemaphoreType.DMA((4,)),
            pltpu.SemaphoreType.DMA((4,)),
            pltpu.SemaphoreType.DMA((4,)),
            pltpu.SemaphoreType.DMA((halves + 3,)),
        ],
        compiler_params=pltpu.CompilerParams(
            collective_id=0, has_side_effects=True, vmem_limit_bytes=VMEM_BYTES
        ),
    )(
        *(
            pltpu.with_memory_space_constraint(array, pltpu.HBM)
            for array in (
                cost_volume.reshape(rows * cols, disparities),
                left_image,
                p_small,
                p_large,
            )
        )
    )
    return total.reshape(rows, cols, disparities)


def solution(mesh):
    in_specs = (P("gy", "gx", None), P("gy", "gx"), P(), P())
    out_specs = P("gy", "gx", None)
    return jax.shard_map(
        on_device, mesh=mesh, in_specs=in_specs, out_specs=out_specs, check_vma=False
    )
```

```python
import functools

import jax
import jax.numpy as jnp
from jax import lax
from jax.experimental import pallas as pl
from jax.experimental.pallas import tpu as pltpu
from jax.sharding import PartitionSpec as P

FAR = 1e30
GRADIENT_GAIN = 4.0
OUT_SCALE = 1.0 / 256.0
LANES = 128
SUBLANES = 8
BATCH = 4
UNROLL = 2
VMEM_BYTES = 20 << 20
MESH = pl.DeviceIdType.MESH


def tree_min(parts):
    parts = list(parts)
    while len(parts) > 1:
        pairs = [jnp.minimum(a, b) for a, b in zip(parts[::2], parts[1::2])]
        parts = pairs + ([parts[-1]] if len(parts) % 2 else [])
    return parts[0]


def all_sublanes_min(x):
    for by in (4, 2, 1):
        x = jnp.minimum(x, pltpu.roll(x, by, 0))
    return x


def kernel(
    rows,
    cols,
    cost_ref,
    image_hbm,
    small_hbm,
    large_hbm,
    out_ref,
    image_ref,
    small_ref,
    large_ref,
    staged,
    ordered,
    order,
    totals,
    costs,
    paths,
    lowests,
    large_lines,
    image_lines,
    outbox,
    inbox,
    edge_out,
    edge_in,
    send_sems,
    recv_sems,
    edge_send_sems,
    edge_recv_sems,
    local_sems,
):
    disparities = cost_ref.shape[1]
    nv = disparities // SUBLANES
    nx, ny = lax.axis_size("gx"), lax.axis_size("gy")
    ix, iy = lax.axis_index("gx"), lax.axis_index("gy")
    lines = (rows, rows, cols, cols)
    lengths = (cols, cols, rows, rows)
    backward = (False, True, False, True)
    targets = (
        {"gx": ix + 1},
        {"gx": ix - 1},
        {"gy": iy + 1},
        {"gy": iy - 1},
    )
    has_next = (ix < nx - 1, ix > 0, iy < ny - 1, iy > 0)
    has_prev = (ix > 0, ix < nx - 1, iy > 0, iy < ny - 1)

    halves = disparities // LANES

    def cost_copy(h):
        return pltpu.make_async_copy(
            cost_ref.at[:, pl.ds(h * LANES, LANES)], staged.at[h], local_sems.at[h]
        )

    small_copies = [
        pltpu.make_async_copy(source, target, local_sems.at[halves + at])
        for at, (source, target) in enumerate(
            ((image_hbm, image_ref), (small_hbm, small_ref), (large_hbm, large_ref))
        )
    ]
    for h in range(halves):
        cost_copy(h).start()
    for copy in small_copies:
        copy.start()

    barrier = pltpu.get_barrier_semaphore()
    for k in range(4):

        @pl.when(has_next[k])
        def _(k=k):
            pl.semaphore_signal(barrier, inc=1, device_id=targets[k], device_id_type=MESH)

    neighbours = sum(jnp.where(flag, 1, 0) for flag in has_next)

    shape = (disparities, disparities)
    source = lax.broadcasted_iota(jnp.int32, shape, 0)
    target = lax.broadcasted_iota(jnp.int32, shape, 1)
    wanted = target // SUBLANES + nv * (target % SUBLANES)
    order[...] = jnp.where(source == wanted, 1.0, 0.0).astype(jnp.bfloat16)

    for copy in small_copies:
        copy.wait()
    image = image_ref[...]
    image_lines[...] = jnp.zeros_like(image_lines)
    image_lines[0, :cols, :rows] = image.T
    image_lines[1, :rows, :cols] = image
    edge_out[...] = jnp.zeros_like(edge_out)
    for k in range(4):
        last = 0 if backward[k] else lengths[k] - 1
        edge_out[k, 0:1, :] = image_lines[k // 2, last : last + 1, :]

    def edge_copy(k):
        return pltpu.make_async_remote_copy(
            src_ref=edge_out.at[k],
            dst_ref=edge_in.at[k],
            send_sem=edge_send_sems.at[k],
            recv_sem=edge_recv_sems.at[k],
            device_id=targets[k],
            device_id_type=MESH,
        )

    def path_copy(k):
        return pltpu.make_async_remote_copy(
            src_ref=outbox.at[k],
            dst_ref=inbox.at[k],
            send_sem=send_sems.at[k],
            recv_sem=recv_sems.at[k],
            device_id=targets[k],
            device_id_type=MESH,
        )

    for h in range(halves):
        cost_copy(h).wait()

    block = jnp.concatenate([staged[h] for h in range(halves)], axis=1)
    block = block.astype(jnp.float32).astype(jnp.bfloat16)
    block = jnp.dot(block, order[...], preferred_element_type=jnp.float32)
    for h in range(halves):
        ordered[h] = block[:, h * LANES : (h + 1) * LANES]

    def turn_in(axis, line, at, count):
        per = LANES // SUBLANES
        for h in range(halves):
            block = ordered[h, at, :].T.reshape(per, SUBLANES, count)
            costs[axis, line, h * per : (h + 1) * per, :, :count] = block

    def turn_across(index, carry):
        for slot in range(BATCH):
            line = index * BATCH + slot
            turn_in(0, line, pl.ds(line, rows, stride=cols), rows)
        return carry

    def turn_down(index, carry):
        for slot in range(BATCH):
            line = index * BATCH + slot
            turn_in(1, line, pl.ds(pl.multiple_of(line * cols, cols), cols), cols)
        return carry

    lax.fori_loop(0, cols // BATCH, turn_across, 0)

    pl.semaphore_wait(barrier, neighbours)
    for k in range(4):

        @pl.when(has_next[k])
        def _(k=k):
            edge_copy(k).start()

    sub = lax.broadcasted_iota(jnp.int32, (SUBLANES, LANES), 0)
    lane = lax.broadcasted_iota(jnp.int32, (SUBLANES, LANES), 1)

    def turn_back(registers, count):
        per = LANES // SUBLANES
        return [
            jnp.concatenate(registers[h * per : (h + 1) * per], axis=0)[:, :count].T
            for h in range(halves)
        ]

    def task(k):
        axis = k // 2
        length, width = lengths[k], lines[k]
        group = LANES // width
        small = small_ref[k].astype(jnp.float32)
        large = large_ref[k].astype(jnp.float32)
        own = image_lines[axis, :length, :]

        @pl.when(has_prev[k])
        def _():
            edge_copy(k).wait_recv()

        @pl.when(jnp.logical_not(has_prev[k]))
        def _():
            edge_in[k] = jnp.zeros((SUBLANES, LANES), jnp.float32)
            inbox[k] = jnp.zeros(inbox.shape[1:], jnp.float32)

        edge = edge_in[k, 0:1, :]
        if backward[k]:
            before = jnp.concatenate([own[1:], edge], axis=0)
        else:
            before = jnp.concatenate([edge, own[:-1]], axis=0)
        large_lines[k] = small + (large - small) / (1.0 + GRADIENT_GAIN * jnp.abs(own - before))

        @pl.when(has_prev[k])
        def _():
            path_copy(k).wait_recv()

        state = []
        for v in range(nv):
            packed = inbox[k, v // group]
            shift = (v % group) * width
            state.append(pltpu.roll(packed, LANES - shift, 1) if shift else packed)

        def step(index, state):
            line = length - 1 - index if backward[k] else index
            capped = large_lines[k, pl.ds(line, SUBLANES, stride=0), :]
            lowest = all_sublanes_min(tree_min(state))
            capped = capped + lowest
            under = jnp.where(sub == 0, FAR, pltpu.roll(state[-1], 1, 0))
            over = jnp.where(sub == SUBLANES - 1, FAR, pltpu.roll(state[0], SUBLANES - 1, 0))
            fresh = []
            for v in range(nv):
                low = state[v - 1] if v else under
                high = state[v + 1] if v < nv - 1 else over
                near = jnp.minimum(state[v], jnp.minimum(low, high) + small)
                fresh.append(costs[axis, line, v] + jnp.minimum(near, capped))
            for v in range(nv):
                paths[k, line, v] = fresh[v]
            lowests[k, line] = lowest
            return tuple(fresh)

        def steps(index, state):
            for part in range(UNROLL):
                state = step(index * UNROLL + part, state)
            return state

        state = lax.fori_loop(0, length // UNROLL, steps, tuple(state))

        @pl.when(has_next[k])
        def _():
            above = lowests[k, 0 if backward[k] else length - 1]
            sent = [part - above for part in state]
            for slot in range(nv // group):
                packed = sent[slot * group]
                for g in range(1, group):
                    moved = pltpu.roll(sent[slot * group + g], g * width, 1)
                    packed = jnp.where(lane >= g * width, moved, packed)
                outbox[k, slot] = packed
            path_copy(k).start()

    def both_ways(k, line, count):
        above = lowests[k, line] + lowests[k + 1, line]
        return turn_back(
            [paths[k, line, v] + paths[k + 1, line, v] - above for v in range(nv)], count
        )

    def down_total(index, carry):
        for slot in range(BATCH):
            line = index * BATCH + slot
            at = pl.ds(pl.multiple_of(line * cols, cols), cols)
            for h, part in enumerate(both_ways(2, line, cols)):
                totals[1, h, at, :] = part
        return carry

    def across_total(index, carry):
        for slot in range(BATCH):
            line = index * BATCH + slot
            at = pl.ds(line, rows, stride=cols)
            for h, part in enumerate(both_ways(0, line, rows)):
                totals[0, h, at, :] = part
        return carry

    low_turn = jnp.minimum(ix, nx - 1 - ix)
    high_turn = jnp.maximum(ix, nx - 1 - ix)
    spare = jnp.where(low_turn >= 3, low_turn - 1, 2 * nx + 2 * ny)

    def one_turn(turn, carry):
        pl.when(turn == ix)(lambda: task(0))
        pl.when(turn == nx - 1 - ix)(lambda: task(1))
        taken = jnp.logical_or(turn == low_turn, turn == high_turn)
        taken = jnp.logical_or(taken, turn == spare)
        used = sum(jnp.where(at < turn, 1, 0) for at in (low_turn, high_turn, spare))
        free = jnp.where(taken, -1, turn - used)
        pl.when(free == 0)(lambda: lax.fori_loop(0, rows // BATCH, turn_down, None))
        pl.when(free == iy)(lambda: task(2))
        pl.when(free == ny - 1 - iy)(lambda: task(3))
        pl.when(free == ny)(lambda: lax.fori_loop(0, rows // BATCH, down_total, None))
        return carry

    lax.fori_loop(0, max(nx, ny + 4), one_turn, 0)
    lax.fori_loop(0, cols // BATCH, across_total, 0)
    rest = jnp.concatenate([totals[0, h] + totals[1, h] for h in range(halves)], axis=1)
    rest = rest * OUT_SCALE
    result = None
    for part in range(3):
        piece = rest.astype(jnp.bfloat16)
        moved = lax.dot_general(
            piece, order[...], (((1,), (1,)), ((), ())), preferred_element_type=jnp.float32
        )
        result = moved if part == 0 else result + moved
        if part < 2:
            rest = rest - piece.astype(jnp.float32)
    out_ref[...] = result

    for k in range(4):

        @pl.when(has_next[k])
        def _(k=k):
            edge_copy(k).wait_send()
            path_copy(k).wait_send()


def on_device(cost_volume, left_image, p_small, p_large):
    rows, cols, disparities = cost_volume.shape
    nv = disparities // SUBLANES
    longest = max(rows, cols)
    packed = nv * longest // LANES
    halves = disparities // LANES
    hbm = pl.BlockSpec(memory_space=pltpu.HBM)
    vmem = pl.BlockSpec(memory_space=pltpu.VMEM)
    total = pl.pallas_call(
        functools.partial(kernel, rows, cols),
        out_shape=jax.ShapeDtypeStruct((rows * cols, disparities), jnp.float32),
        in_specs=[hbm] * 4,
        out_specs=vmem,
        scratch_shapes=[
            pltpu.VMEM((rows, cols), jnp.float32),
            pltpu.SMEM((4,), jnp.int32),
            pltpu.SMEM((4,), jnp.int32),
            pltpu.VMEM((halves, rows * cols, LANES), jnp.int32),
            pltpu.VMEM((halves, rows * cols, LANES), jnp.float32),
            pltpu.VMEM((disparities, disparities), jnp.bfloat16),
            pltpu.VMEM((2, halves, rows * cols, LANES), jnp.float32),
            pltpu.VMEM((2, longest, nv, SUBLANES, LANES), jnp.float32),
            pltpu.VMEM((4, longest, nv, SUBLANES, LANES), jnp.float32),
            pltpu.VMEM((4, longest, SUBLANES, LANES), jnp.float32),
            pltpu.VMEM((4, longest, LANES), jnp.float32),
            pltpu.VMEM((2, longest, LANES), jnp.float32),
            pltpu.VMEM((4, packed, SUBLANES, LANES), jnp.float32),
            pltpu.VMEM((4, packed, SUBLANES, LANES), jnp.float32),
            pltpu.VMEM((4, SUBLANES, LANES), jnp.float32),
            pltpu.VMEM((4, SUBLANES, LANES), jnp.float32),
            pltpu.SemaphoreType.DMA((4,)),
            pltpu.SemaphoreType.DMA((4,)),
            pltpu.SemaphoreType.DMA((4,)),
            pltpu.SemaphoreType.DMA((4,)),
            pltpu.SemaphoreType.DMA((halves + 3,)),
        ],
        compiler_params=pltpu.CompilerParams(
            collective_id=0, has_side_effects=True, vmem_limit_bytes=VMEM_BYTES
        ),
    )(
        *(
            pltpu.with_memory_space_constraint(array, pltpu.HBM)
            for array in (
                cost_volume.reshape(rows * cols, disparities),
                left_image,
                p_small,
                p_large,
            )
        )
    )
    return total.reshape(rows, cols, disparities)


def solution(mesh):
    in_specs = (P("gy", "gx", None), P("gy", "gx"), P(), P())
    out_specs = P("gy", "gx", None)
    return jax.shard_map(
        on_device, mesh=mesh, in_specs=in_specs, out_specs=out_specs, check_vma=False
    )
```
